32 devices in a mesh: groups: 2 (over y), dp: 4 (over z), expert: 4 (over x, core).
Axes of the slice: x: 2, y: 2, z: 4, core: 2. Of those that a mesh axis runs over, the one named last changes fastest.
Arguments:
- tokens: bfloat16 [4096, 3072], P(('groups', 'dp', 'expert')), parts along dimension 0, may hold values from -6 to 6
- route: int32 [4096, 1], P(('groups', 'dp', 'expert')), parts along dimension 0, may hold values from 0 to 3; in each aligned block of 128 rows (0 to 127, 128 to 255, ...) at most 36 rows name the same one
- w_up: bfloat16 [4, 3072, 8192], P('expert', None, 'dp'), may hold values from -0.109375 to 0.109375
- grad_up: bfloat16 [4096, 8192], P(('groups', 'dp', 'expert')), parts along dimension 0, may hold values from -6 to 6
Outputs:
- up_out: bfloat16 [4096, 8192], P(('groups', 'dp', 'expert')), parts along dimension 0
- grad_w: bfloat16 [8, 3072, 8192], P(('groups', 'expert'), None, 'dp'), parts along dimension 0
The draws below stay inside these ranges and needn't reach their ends.
There are 2 independent parts, one for each index of `groups`. The reference program is written for one: setup_inputs(seed, part) draws one part's arguments, and reference() takes and returns one part's arrays. A program takes and returns all parts, laid end to end along the dimension named above; an argument that names none is the same for every part. Nothing has to cross between parts.
Inputs may be any that keep to these rules, and one draw needn't show every extreme that they name: `route`: in each aligned block of 128 rows (the rows of one device) no expert is named by more than 36 rows; in every draw some block names some expert exactly 36 times.
All inputs are finite; a program needn't handle non-finite values.
Results may differ from the reference program's by a relative error of at most 0.001.
Values may be sent and summed in bfloat16 or wider, within the bound.
A program may use at most 128 MiB of HBM per device.

```python
import math
import jax
import jax.numpy as jnp
import numpy as np
from jax import lax

D = 3072
FF = 8192
ROWS_DEV = 128
EXPERTS = 4
CAP = 36
ROWS = 2048


def levels(own_key, shape, shards, least, high):
    loudness = 1.0
    for position, parts in shards:
        steps = jax.random.uniform(jax.random.fold_in(jax.random.fold_in(own_key, 6), position), (parts,), jnp.float32, least / len(shards), high / len(shards))
        loudness = loudness * jnp.repeat(jnp.exp(steps), shape[position] // parts).reshape((-1,) + (1,) * (len(shape) - 1 - position))
    return loudness


def deal_out(own_key, own, number, rows, count, top, most, lean):
    ranking = jax.random.permutation(own_key, count)
    packed, usual = load_shares(count, rows * top, most, lean, True), load_shares(count, rows * top, most, lean, False)
    places = jnp.arange(count)

    def named(tallies, offset_by):
        used = int((tallies > 0).sum())
        fixed = max(1, used // 4)
        passed = fixed + (places - fixed + offset_by * (used - fixed)) % max(1, count - fixed)
        return jnp.zeros((count,), jnp.int32).at[ranking[jnp.where(places < fixed, places, passed)]].set(jnp.asarray(tallies, jnp.int32))

    tallies = jnp.where(number % 4 == 0, named(packed, number // 4), named(usual, number - number // 4 - 1))
    mixed = jax.random.permutation(jax.random.fold_in(own, 3), count)
    giver, taker = mixed[0:count // 2 * 2:2], mixed[1:count // 2 * 2:2]
    margin = jnp.minimum(tallies[giver] - 1, most - tallies[taker]) // 2
    margin = jnp.where((giver == ranking[0]) | (taker == ranking[0]) | (tallies[taker] == 0), 0, jnp.maximum(margin, 0))
    passed = jax.random.randint(jax.random.fold_in(own, 4), (count // 2,), 0, 1 << 20) % (margin + 1)
    tallies = tallies.at[giver].add(-passed).at[taker].add(passed)
    labels = jnp.searchsorted(jnp.cumsum(tallies), jnp.arange(rows * top), side="right").astype(jnp.int32)
    listing = labels.reshape(top, rows).T
    listing = listing[jax.random.permutation(jax.random.fold_in(own, 1), rows)]
    offset_by = jax.random.randint(jax.random.fold_in(own, 2), (rows, 1), 0, top)
    return jnp.take_along_axis(listing, (jnp.arange(top)[None, :] + offset_by) % top, axis=1)


def load_shares(number_of, total, bound, skew, full):
    loads = [(1 << 20) // math.isqrt(standing ** skew) + 1 for standing in range(1, number_of + 1)]
    largest = bound if full else min(bound, max(-(-total // number_of), total * loads[0] // sum(loads)))
    least = 1 if total - largest >= number_of - 1 else 0
    given, spare = [largest] + [least] * (number_of - 1), total - largest - least * (number_of - 1)
    while spare > 0:
        free = [i for i in range(1, number_of) if given[i] < largest] or [i for i in range(1, number_of) if given[i] < bound]
        pool, left = sum([loads[i] for i in free]), spare
        for i in free:
            extra = min(bound - given[i], max(1, left * loads[i] // pool), spare)
            given[i] = given[i] + extra
            spare = spare - extra
    return np.array(given)


def gaussian(rng, dims, width, reach, shards=(), kind=jnp.bfloat16):
    array = jax.random.normal(rng, dims, jnp.float32) * width
    if len(shards) > 0:
        array = levels(rng, dims, shards, -0.22, 0.18) * array
    return jnp.clip(array, min=-reach, max=reach).astype(kind)


def setup_inputs(seed: int = 0, part: int = 0) -> dict:
    splits = jax.random.split(jax.random.key(seed), 5)
    own_keys = jax.random.split(jax.random.fold_in(splits[4], part), 5)
    tokens = gaussian(own_keys[0], (ROWS, D), 1.0, 6.0, ((0, 16),))
    route_keys = jax.random.split(jax.random.fold_in(own_keys[1], 1), ROWS // ROWS_DEV)
    route_turns = jax.random.permutation(jax.random.fold_in(own_keys[1], 3), ROWS // ROWS_DEV)
    route = jax.vmap(lambda own, number: deal_out(jax.random.fold_in(own_keys[1], 2), own, number, ROWS_DEV, EXPERTS, 1, CAP, 2))(route_keys, route_turns).reshape((ROWS, 1))
    w_up = gaussian(splits[2], (EXPERTS, D, FF), D ** -0.5, 0.109375, ((0, 4), (2, 4)))
    grad_up = gaussian(own_keys[3], (ROWS, FF), 1.0, 6.0, ((0, 16),))
    return {"tokens": tokens, "route": route, "w_up": w_up, "grad_up": grad_up}


def reference(tokens, route, w_up, grad_up):
    experts = w_up.shape[0]
    routed = route[:, 0]
    limit = CAP * tokens.shape[0] // ROWS_DEV

    def one_expert(carry, expert):
        order = jnp.argsort((routed != expert).astype(jnp.int32), stable=True)[:limit].astype(jnp.int32)
        live = (routed[order] == expert)[:, None]
        chosen = jnp.where(live, tokens[order], jnp.zeros((), jnp.bfloat16))
        weight = lax.dynamic_index_in_dim(w_up, expert, 0, keepdims=False)
        output = jnp.dot(chosen, weight, preferred_element_type=jnp.float32).astype(jnp.bfloat16)
        output = jnp.where(live, output, jnp.zeros((), jnp.bfloat16))
        cotangent = grad_up[order]
        gradient = jnp.dot(chosen.T, cotangent, preferred_element_type=jnp.float32).astype(jnp.bfloat16)
        return carry.at[order].add(output), gradient

    start_rows = jnp.zeros((tokens.shape[0], w_up.shape[2]), jnp.bfloat16)
    up_out, grad_w = lax.scan(one_expert, start_rows, jnp.arange(experts, dtype=jnp.int32))
    return up_out, grad_w
```

```python
import functools

import jax
import jax.numpy as jnp
from jax import lax
from jax.experimental import pallas as pl
from jax.experimental.pallas import tpu as pltpu
from jax.sharding import PartitionSpec as P

MESH = pl.DeviceIdType.MESH
BF16 = jnp.bfloat16
F32 = jnp.float32
H = 2
LATE = 2


def chunk_of(width):
    return 512 if width % 512 == 0 else width


def flat(ref, first, count, cols):
    return ref[pl.ds(first // 8, count // 8), :, cols].reshape(count, -1)


def gradient(X, Gx, first, gw, after=None):
    rows, F = gw.shape
    K = X.shape[0] * 8
    tm = 256 if rows % 256 == 0 else rows
    step = chunk_of(F)

    def body(i, _):
        at = pl.ds(pl.multiple_of(i * tm, tm), tm)
        xt = flat(X, 0, K, pl.ds(pl.multiple_of(first + i * tm, 128), tm)).T
        for n in range(F // step):
            cols = slice(n * step, (n + 1) * step)
            gw[at, cols] = jnp.dot(xt, flat(Gx, 0, K, cols), preferred_element_type=F32).astype(BF16)
        if after is not None:
            after(i)
        return 0

    lax.fori_loop(0, rows // tm, body, 0)


def plans(Z):
    if Z == 4:
        texts = (
            "R0G0P0R1J0P1B0S1s1J1R2P2S2s2B1G1J2S3s3G2B2R3P3J3G3B3",
            "R0P0J0S1s1G0R1P1S2s2R2B0P2S3s3R3J1J2B1P3B2G1G2J3B3G3",
        )
        return [[(text[i], int(text[i + 1])) for i in range(0, len(text), 2)] for text in texts]
    plan = [(name, 0) for name in "RPJGB"]
    for k in range(1, Z):
        plan += [(name, k) for name in "RSsPJB"]
    plan += [("G", k) for k in range(1, Z)]
    return [plan, plan]


def kernel(
    Z, E, C,
    tokens, route, w_hbm, grads,
    out, gw, X, Gx,
    tok, tgt, gz, w, Yx, psend, gsend, ysend, usend, rv,
    tok_ss, tok_rs, tgt_ss, tgt_rs, gz_ss, gz_rs,
    x_ss, x_rs, g_ss, g_rs, y_ss, y_rs, u_ss, u_rs, loc, wsem,
):
    R, D = tokens.shape
    F = w_hbm.shape[1]
    RH = R // H
    d = lax.axis_index("dp")
    me = lax.axis_index("expert")
    EC = E * C
    T = C // 8
    low = jnp.minimum(d, Z - 1 - d)
    inner = low > 0

    def block(k):
        if k == 0:
            return d
        near = d + (k + 1) // 2 if k % 2 else d - k // 2
        far = jnp.where(d <= Z - 1 - d, k, Z - 1 - k)
        return jnp.where(k <= 2 * low, near, far)

    rcopy = pltpu.make_async_copy(route, rv, wsem.at[1])
    rcopy.start()
    owntok = pltpu.make_async_copy(tokens, tok.at[d], wsem.at[2])
    owntok.start()

    barrier = pltpu.get_barrier_semaphore()
    for j in range(1, Z):
        pl.semaphore_signal(barrier, inc=1, device_id={"dp": lax.rem(d + j, Z)}, device_id_type=MESH)
    for j in range(1, E):
        pl.semaphore_signal(barrier, inc=1, device_id={"expert": lax.rem(me + j, E)}, device_id_type=MESH)
    pl.semaphore_wait(barrier, Z - 1 + E - 1)

    def half(h):
        return pl.ds(h * RH, RH)

    def tok_copy(src, b, h, side):
        return pltpu.make_async_remote_copy(
            src_ref=src.at[half(h)], dst_ref=tok.at[b, half(h)],
            send_sem=tok_ss.at[b, h, side], recv_sem=tok_rs.at[b, h],
            device_id={"dp": d - 1 if side == 0 else d + 1}, device_id_type=MESH)

    for h in range(H):
        @pl.when(d > 0)
        def _():
            tok_copy(tokens, d, h, 0).start()

        @pl.when(d < Z - 1)
        def _():
            tok_copy(tokens, d, h, 1).start()

    wcopy = pltpu.make_async_copy(w_hbm, w, wsem.at[0])
    wcopy.start()
    owngrad = pltpu.make_async_copy(grads.at[:, pl.ds(pl.multiple_of(d * F, 128), F)], gz.at[d], wsem.at[3])
    owngrad.start()

    rcopy.wait()
    row = jnp.broadcast_to(rv[...], (R, R))
    ri = lax.broadcasted_iota(jnp.int32, (R, R), 0)
    ci = lax.broadcasted_iota(jnp.int32, (R, R), 1)
    col = jnp.sum(jnp.where(ri == ci, row, 0), axis=1, keepdims=True)
    rank = jnp.sum(jnp.where((col == row) & (ri < ci), 1, 0), axis=0, keepdims=True)
    slot = (rv[...] * C + rank).astype(F32)
    tgt[d] = jnp.broadcast_to(slot, (8, R))

    def tgt_copy(j):
        return pltpu.make_async_remote_copy(
            src_ref=tgt.at[d], dst_ref=tgt.at[d], send_sem=tgt_ss.at[j], recv_sem=tgt_rs.at[d],
            device_id={"dp": lax.rem(d + j, Z)}, device_id_type=MESH)

    for j in range(1, Z):
        tgt_copy(j).start()

    def one_hot(b):
        t = tgt[b][0:1].astype(jnp.int32)
        s = lax.broadcasted_iota(jnp.int32, (EC, R), 0)
        return jnp.where(s == t, 1.0, 0.0).astype(BF16)

    def receive(k):
        if k == 0:
            owntok.wait()
            return
        b = block(k)
        for h in range(H):
            piece = tok.at[b, half(h)]
            pltpu.make_async_copy(piece, piece, tok_rs.at[b, h]).wait()

            @pl.when((b < d) & (d < Z - 1))
            def _():
                tok_copy(tok.at[b], b, h, 1).start()

            @pl.when((b > d) & (d > 0))
            def _():
                tok_copy(tok.at[b], b, h, 0).start()
        pltpu.make_async_copy(tgt.at[b], tgt.at[b], tgt_rs.at[b]).wait()

    def gz_copy(k, h):
        to = block(k)
        rows = pl.ds(h * (R // 2), R // 2)
        return pltpu.make_async_remote_copy(
            src_ref=grads.at[rows, pl.ds(pl.multiple_of(to * F, 128), F)], dst_ref=gz.at[d, rows],
            send_sem=gz_ss.at[k, h], recv_sem=gz_rs.at[d, h], device_id={"dp": to}, device_id_type=MESH)

    def rows_at(b, e):
        return pl.ds((b * E + e) * T, T)

    def plane_copy(send, k, j, dst, b, ss, rs):
        to = lax.rem(me + j, E)
        if j == 0:
            return pltpu.make_async_copy(send.at[k % 2, to], dst.at[rows_at(b, me)], rs.at[b, 0])
        return pltpu.make_async_remote_copy(
            src_ref=send.at[k % 2, to], dst_ref=dst.at[rows_at(b, me)],
            send_sem=ss.at[k % 2, j], recv_sem=rs.at[b, j], device_id={"expert": to}, device_id_type=MESH)

    def plane_send(send, k, dst, ss, rs):
        for j in list(range(1, E)) + [0]:
            plane_copy(send, k, j, dst, block(k), ss, rs).start()

    def plane_drain(send, k, dst, ss, rs):
        for j in range(1, E):
            plane_copy(send, k, j, dst, block(k), ss, rs).wait_send()

    def plane_arrived(k, dst, rs, offsets=None):
        b = block(k)
        for j in offsets or range(E):
            piece = dst.at[rows_at(b, 0)]
            pltpu.make_async_copy(piece, piece, rs.at[b, j]).wait()

    def pack(src, b, send, k):
        oh = one_hot(b)
        width = src.shape[-1]
        step = chunk_of(width)

        def body(i, _):
            cols = pl.ds(pl.multiple_of(i * step, step), step)
            r = jnp.dot(oh, src[b, :, cols], preferred_element_type=F32)
            for e in range(E):
                send[k % 2, e, :, :, cols] = r[e * C:(e + 1) * C].astype(BF16).reshape(T, 8, -1)
            return 0

        lax.fori_loop(0, width // step, body, 0)

    def pack_tokens(k):
        if k >= 2:
            plane_drain(psend, k - 2, X, x_ss, x_rs)
        pack(tok, block(k), psend, k)
        plane_send(psend, k, X, x_ss, x_rs)

    def project(k):
        b = block(k)
        plane_arrived(k, X, x_rs)
        if k >= 2:
            plane_drain(ysend, k - 2, Yx, y_ss, y_rs)
        if k == 0:
            wcopy.wait()
        step = chunk_of(F)

        def body(i, _):
            cols = pl.ds(pl.multiple_of(i * step, step), step)
            r = jnp.dot(flat(X, b * EC, EC, slice(None)), w[:, cols], preferred_element_type=F32)
            for e in range(E):
                ysend[k % 2, e, :, :, cols] = r[e * C:(e + 1) * C].astype(BF16).reshape(T, 8, -1)
            return 0

        lax.fori_loop(0, F // step, body, 0)
        plane_send(ysend, k, Yx, y_ss, y_rs)

    def u_copy(k):
        b = block(k)
        cols = pl.ds(pl.multiple_of(d * F, 128), F)
        if k == 0:
            return pltpu.make_async_copy(usend.at[0], out.at[:, cols], loc.at[0])
        return pltpu.make_async_remote_copy(
            src_ref=usend.at[k], dst_ref=out.at[:, cols], send_sem=u_ss.at[k], recv_sem=u_rs.at[d],
            device_id={"dp": b}, device_id_type=MESH)

    def give_back(k):
        b = block(k)
        plane_arrived(k, Yx, y_rs)
        oh = one_hot(b)
        step = chunk_of(F)

        def body(i, _):
            cols = pl.ds(pl.multiple_of(i * step, step), step)
            r = lax.dot_general(oh, flat(Yx, b * EC, EC, cols), (((0,), (0,)), ((), ())), preferred_element_type=F32)
            usend[k, :, cols] = r.astype(BF16)
            return 0

        lax.fori_loop(0, F // step, body, 0)
        u_copy(k).start()

    def pack_grads(k):
        b = block(k)
        if k == 0:
            owngrad.wait()
        else:
            for h in range(2):
                piece = gz.at[b, pl.ds(h * (R // 2), R // 2)]
                pltpu.make_async_copy(piece, piece, gz_rs.at[b, h]).wait()
        if k >= 2:
            plane_drain(gsend, k - 2, Gx, g_ss, g_rs)
            plane_arrived(k - 2, Gx, g_rs, (0,))
        pack(gz, b, gsend, k)
        plane_send(gsend, k, Gx, g_ss, g_rs)

    steps = {
        "R": receive, "P": pack_tokens, "J": project, "B": give_back, "G": pack_grads,
        "S": lambda k: gz_copy(k, 0).start(), "s": lambda k: gz_copy(k, 1).start(),
    }

    def follow(plan):
        for name, k in plan:
            steps[name](k)

    ends, middle = plans(Z)
    if ends == middle:
        follow(ends)
    else:
        pl.when(~inner)(lambda: follow(ends))
        pl.when(inner)(lambda: follow(middle))

    for send, dst, ss, rs in ((psend, X, x_ss, x_rs), (gsend, Gx, g_ss, g_rs), (ysend, Yx, y_ss, y_rs)):
        for k in range(max(Z - 2, 0), Z):
            plane_drain(send, k, dst, ss, rs)
    for k in range(Z):
        plane_arrived(k, Gx, g_rs, range(0 if k >= Z - 2 else 1, E))
    gradient(X, Gx, 0, gw)

    for h in range(H):
        @pl.when(d > 0)
        def _():
            tok_copy(tokens, d, h, 0).wait_send()

        @pl.when(d < Z - 1)
        def _():
            tok_copy(tokens, d, h, 1).wait_send()

        for k in range(1, Z):
            b = block(k)

            @pl.when((b < d) & (d < Z - 1))
            def _():
                tok_copy(tok.at[b], b, h, 1).wait_send()

            @pl.when((b > d) & (d > 0))
            def _():
                tok_copy(tok.at[b], b, h, 0).wait_send()

    for k in range(1, Z):
        tgt_copy(k).wait_send()
        for h in range(2):
            gz_copy(k, h).wait_send()
    u_copy(0).wait()
    for k in range(1, Z):
        u_copy(k).wait_send()
        b = block(k)
        piece = out.at[:, pl.ds(pl.multiple_of(b * F, 128), F)]
        pltpu.make_async_copy(piece, piece, u_rs.at[b]).wait()


def place(n, rows_in, gw_in, X, Gx, rows_out, gw_out, rest, sems):
    head, F = gw_in.shape
    step = head // n
    copies = []
    for i in range(n):
        part = pl.ds(i * step, step)
        copies.append(pltpu.make_async_copy(gw_in.at[part], gw_out.at[part], sems.at[i]))
    copies.append(pltpu.make_async_copy(rows_in, rows_out, sems.at[n]))
    for copy in copies:
        copy.start()
    tm = 256
    tail = [
        pltpu.make_async_copy(rest.at[pl.ds(i * tm, tm)], gw_out.at[pl.ds(head + i * tm, tm)], sems.at[n + 1 + i])
        for i in range(rest.shape[0] // tm)
    ]
    for i, copy in enumerate(tail):
        gradient(X, Gx, head + i * tm, rest.at[pl.ds(i * tm, tm)])
        copy.start()
    for copy in copies + tail:
        copy.wait()


def local(Z, E, tokens, route, w_up, grad_up):
    R, D = tokens.shape
    w = w_up[0]
    F = w.shape[1]
    FF = grad_up.shape[1]
    C = -(-(9 * R // (8 * E)) // 8) * 8
    EC = E * C
    dma = pltpu.SemaphoreType.DMA
    any_spec = pl.BlockSpec(memory_space=pl.ANY)
    flops = 4 * Z * EC * D * F
    vmem = pl.BlockSpec(memory_space=pltpu.VMEM)
    late = LATE * 256
    out, gw, X, Gx = pl.pallas_call(
        functools.partial(kernel, Z, E, C),
        out_shape=(
            pltpu.VMEM((R, FF), BF16),
            pltpu.VMEM((D - late, F), BF16),
            pltpu.VMEM((Z * EC // 8, 8, D), BF16),
            pltpu.VMEM((Z * EC // 8, 8, F), BF16),
        ),
        in_specs=[any_spec] * 4,
        out_specs=(any_spec, vmem, vmem, vmem),
        scratch_shapes=[
            pltpu.VMEM((Z, R, D), BF16),
            pltpu.VMEM((Z, 8, R), F32),
            pltpu.VMEM((Z, R, F), BF16),
            pltpu.VMEM((D, F), BF16),
            pltpu.VMEM((Z * EC // 8, 8, F), BF16),
            pltpu.VMEM((2, E, C // 8, 8, D), BF16),
            pltpu.VMEM((2, E, C // 8, 8, F), BF16),
            pltpu.VMEM((2, E, C // 8, 8, F), BF16),
            pltpu.VMEM((Z, R, F), BF16),
            pltpu.VMEM((1, R), jnp.int32),
            dma((Z, H, 2)), dma((Z, H)), dma((Z,)), dma((Z,)), dma((Z, 2)), dma((Z, 2)),
            dma((2, E)), dma((Z, E)), dma((2, E)), dma((Z, E)), dma((2, E)), dma((Z, E)),
            dma((Z,)), dma((Z,)), dma((1,)), dma((4,)),
        ],
        compiler_params=pltpu.CompilerParams(
            collective_id=0, has_side_effects=True, vmem_limit_bytes=36 * 1024 * 1024
        ),
        cost_estimate=pl.CostEstimate(flops=flops, bytes_accessed=2 * D * F, transcendentals=0),
    )(*(pltpu.with_memory_space_constraint(a, pltpu.HBM) for a in (tokens, route.reshape(1, R), w, grad_up)))
    parts = 8
    rows, grad = pl.pallas_call(
        functools.partial(place, parts),
        out_shape=(jax.ShapeDtypeStruct((R, FF), BF16), jax.ShapeDtypeStruct((D, F), BF16)),
        in_specs=[any_spec, any_spec, vmem, vmem],
        out_specs=(any_spec, any_spec),
        scratch_shapes=[pltpu.VMEM((late, F), BF16), dma((parts + 1 + LATE,))],
        compiler_params=pltpu.CompilerParams(vmem_limit_bytes=16 * 1024 * 1024),
    )(*(pltpu.with_memory_space_constraint(a, pltpu.VMEM) for a in (out, gw, X, Gx)))
    return rows, grad[None]


def solution(mesh):
    rows = P(("groups", "dp", "expert"), None)
    return jax.shard_map(
        functools.partial(local, mesh.shape["dp"], mesh.shape["expert"]),
        mesh=mesh,
        in_specs=(rows, rows, P("expert", None, "dp"), rows),
        out_specs=(rows, P(("groups", "expert"), None, "dp")),
        check_vma=False,
    )
```

```python
import functools

import jax
import jax.numpy as jnp
from jax import lax
from jax.experimental import pallas as pl
from jax.experimental.pallas import tpu as pltpu
from jax.sharding import PartitionSpec as P

MESH = pl.DeviceIdType.MESH
BF16 = jnp.bfloat16
F32 = jnp.float32
H = 2
LATE = 5


def chunk_of(width):
    return 512 if width % 512 == 0 else width


def flat(ref, first, count, cols):
    return ref[pl.ds(first // 8, count // 8), :, cols].reshape(count, -1)


def gradient(X, Gx, first, gw, after=None):
    rows, F = gw.shape
    K = X.shape[0] * 8
    tm = 256 if rows % 256 == 0 else rows
    step = chunk_of(F)

    def body(i, _):
        at = pl.ds(pl.multiple_of(i * tm, tm), tm)
        xt = flat(X, 0, K, pl.ds(pl.multiple_of(first + i * tm, 128), tm)).T
        for n in range(F // step):
            cols = slice(n * step, (n + 1) * step)
            gw[at, cols] = jnp.dot(xt, flat(Gx, 0, K, cols), preferred_element_type=F32).astype(BF16)
        if after is not None:
            after(i)
        return 0

    lax.fori_loop(0, rows // tm, body, 0)


def plans(Z):
    if Z == 4:
        texts = (
            "R0G0P0R1J0P1B0S1s1J1R2P2S2s2B1G1J2S3s3G2B2R3P3J3G3B3",
            "R0P0J0S1s1G0R1P1S2R2s2B0P2S3s3R3J1J2B1P3B2G1G2J3B3G3",
        )
        return [[(text[i], int(text[i + 1])) for i in range(0, len(text), 2)] for text in texts]
    plan = [(name, 0) for name in "RPJGB"]
    for k in range(1, Z):
        plan += [(name, k) for name in "RSsPJB"]
    plan += [("G", k) for k in range(1, Z)]
    return [plan, plan]


def kernel(
    Z, E, C,
    tokens, route, w_hbm, grads,
    out, gw, X, Gx,
    tok, tgt, gz, w, Yx, psend, gsend, ysend, usend, rv,
    tok_ss, tok_rs, tgt_ss, tgt_rs, gz_ss, gz_rs,
    x_ss, x_rs, g_ss, g_rs, y_ss, y_rs, u_ss, u_rs, loc, wsem,
):
    R, D = tokens.shape
    F = w_hbm.shape[1]
    RH = R // H
    d = lax.axis_index("dp")
    me = lax.axis_index("expert")
    EC = E * C
    T = C // 8
    low = jnp.minimum(d, Z - 1 - d)
    inner = low > 0

    def block(k):
        if k == 0:
            return d
        near = d + (k + 1) // 2 if k % 2 else d - k // 2
        far = jnp.where(d <= Z - 1 - d, k, Z - 1 - k)
        return jnp.where(k <= 2 * low, near, far)

    rcopy = pltpu.make_async_copy(route, rv, wsem.at[1])
    rcopy.start()
    owntok = pltpu.make_async_copy(tokens, tok.at[d], wsem.at[2])
    owntok.start()

    barrier = pltpu.get_barrier_semaphore()
    for j in range(1, Z):
        pl.semaphore_signal(barrier, inc=1, device_id={"dp": lax.rem(d + j, Z)}, device_id_type=MESH)
    for j in range(1, E):
        pl.semaphore_signal(barrier, inc=1, device_id={"expert": lax.rem(me + j, E)}, device_id_type=MESH)
    pl.semaphore_wait(barrier, Z - 1 + E - 1)

    def half(h):
        return pl.ds(h * RH, RH)

    def tok_copy(src, b, h, side):
        return pltpu.make_async_remote_copy(
            src_ref=src.at[half(h)], dst_ref=tok.at[b, half(h)],
            send_sem=tok_ss.at[b, h, side], recv_sem=tok_rs.at[b, h],
            device_id={"dp": d - 1 if side == 0 else d + 1}, device_id_type=MESH)

    for h in range(H):
        @pl.when(d > 0)
        def _():
            tok_copy(tokens, d, h, 0).start()

        @pl.when(d < Z - 1)
        def _():
            tok_copy(tokens, d, h, 1).start()

    wcopy = pltpu.make_async_copy(w_hbm, w, wsem.at[0])
    wcopy.start()
    owngrad = pltpu.make_async_copy(grads.at[:, pl.ds(pl.multiple_of(d * F, 128), F)], gz.at[d], wsem.at[3])
    owngrad.start()

    rcopy.wait()
    row = jnp.broadcast_to(rv[...], (R, R))
    ri = lax.broadcasted_iota(jnp.int32, (R, R), 0)
    ci = lax.broadcasted_iota(jnp.int32, (R, R), 1)
    col = jnp.sum(jnp.where(ri == ci, row, 0), axis=1, keepdims=True)
    rank = jnp.sum(jnp.where((col == row) & (ri < ci), 1, 0), axis=0, keepdims=True)
    slot = (rv[...] * C + rank).astype(F32)
    tgt[d] = jnp.broadcast_to(slot, (8, R))

    def tgt_copy(j):
        return pltpu.make_async_remote_copy(
            src_ref=tgt.at[d], dst_ref=tgt.at[d], send_sem=tgt_ss.at[j], recv_sem=tgt_rs.at[d],
            device_id={"dp": lax.rem(d + j, Z)}, device_id_type=MESH)

    for j in range(1, Z):
        tgt_copy(j).start()

    def one_hot(b):
        t = tgt[b][0:1].astype(jnp.int32)
        s = lax.broadcasted_iota(jnp.int32, (EC, R), 0)
        return jnp.where(s == t, 1.0, 0.0).astype(BF16)

    def receive(k):
        if k == 0:
            owntok.wait()
            return
        b = block(k)
        for h in range(H):
            piece = tok.at[b, half(h)]
            pltpu.make_async_copy(piece, piece, tok_rs.at[b, h]).wait()

            @pl.when((b < d) & (d < Z - 1))
            def _():
                tok_copy(tok.at[b], b, h, 1).start()

            @pl.when((b > d) & (d > 0))
            def _():
                tok_copy(tok.at[b], b, h, 0).start()
        pltpu.make_async_copy(tgt.at[b], tgt.at[b], tgt_rs.at[b]).wait()

    def gz_copy(k, h):
        to = block(k)
        rows = pl.ds(h * (R // 2), R // 2)
        return pltpu.make_async_remote_copy(
            src_ref=grads.at[rows, pl.ds(pl.multiple_of(to * F, 128), F)], dst_ref=gz.at[d, rows],
            send_sem=gz_ss.at[k, h], recv_sem=gz_rs.at[d, h], device_id={"dp": to}, device_id_type=MESH)

    def rows_at(b, e):
        return pl.ds((b * E + e) * T, T)

    def plane_copy(send, k, j, dst, b, ss, rs):
        to = lax.rem(me + j, E)
        if j == 0:
            return pltpu.make_async_copy(send.at[k % 2, to], dst.at[rows_at(b, me)], rs.at[b, 0])
        return pltpu.make_async_remote_copy(
            src_ref=send.at[k % 2, to], dst_ref=dst.at[rows_at(b, me)],
            send_sem=ss.at[k % 2, j], recv_sem=rs.at[b, j], device_id={"expert": to}, device_id_type=MESH)

    def plane_send(send, k, dst, ss, rs):
        for j in list(range(1, E)) + [0]:
            plane_copy(send, k, j, dst, block(k), ss, rs).start()

    def plane_drain(send, k, dst, ss, rs):
        for j in range(1, E):
            plane_copy(send, k, j, dst, block(k), ss, rs).wait_send()

    def plane_arrived(k, dst, rs, offsets=None):
        b = block(k)
        for j in offsets or range(E):
            piece = dst.at[rows_at(b, 0)]
            pltpu.make_async_copy(piece, piece, rs.at[b, j]).wait()

    def pack(src, b, send, k):
        oh = one_hot(b)
        width = src.shape[-1]
        step = chunk_of(width)

        def body(i, _):
            cols = pl.ds(pl.multiple_of(i * step, step), step)
            r = jnp.dot(oh, src[b, :, cols], preferred_element_type=F32)
            for e in range(E):
                send[k % 2, e, :, :, cols] = r[e * C:(e + 1) * C].astype(BF16).reshape(T, 8, -1)
            return 0

        lax.fori_loop(0, width // step, body, 0)

    def pack_tokens(k):
        if k >= 2:
            plane_drain(psend, k - 2, X, x_ss, x_rs)
        pack(tok, block(k), psend, k)
        plane_send(psend, k, X, x_ss, x_rs)

    def project(k):
        b = block(k)
        plane_arrived(k, X, x_rs)
        if k >= 2:
            plane_drain(ysend, k - 2, Yx, y_ss, y_rs)
        if k == 0:
            wcopy.wait()
        step = chunk_of(F)

        def body(i, _):
            cols = pl.ds(pl.multiple_of(i * step, step), step)
            r = jnp.dot(flat(X, b * EC, EC, slice(None)), w[:, cols], preferred_element_type=F32)
            for e in range(E):
                ysend[k % 2, e, :, :, cols] = r[e * C:(e + 1) * C].astype(BF16).reshape(T, 8, -1)
            return 0

        lax.fori_loop(0, F // step, body, 0)
        plane_send(ysend, k, Yx, y_ss, y_rs)

    def u_copy(k):
        b = block(k)
        cols = pl.ds(pl.multiple_of(d * F, 128), F)
        if k == 0:
            return pltpu.make_async_copy(usend.at[0], out.at[:, cols], loc.at[0])
        return pltpu.make_async_remote_copy(
            src_ref=usend.at[k], dst_ref=out.at[:, cols], send_sem=u_ss.at[k], recv_sem=u_rs.at[d],
            device_id={"dp": b}, device_id_type=MESH)

    def give_back(k):
        b = block(k)
        plane_arrived(k, Yx, y_rs)
        oh = one_hot(b)
        step = chunk_of(F)

        def body(i, _):
            cols = pl.ds(pl.multiple_of(i * step, step), step)
            r = lax.dot_general(oh, flat(Yx, b * EC, EC, cols), (((0,), (0,)), ((), ())), preferred_element_type=F32)
            usend[k, :, cols] = r.astype(BF16)
            return 0

        lax.fori_loop(0, F // step, body, 0)
        u_copy(k).start()

    def pack_grads(k):
        b = block(k)
        if k == 0:
            owngrad.wait()
        else:
            for h in range(2):
                piece = gz.at[b, pl.ds(h * (R // 2), R // 2)]
                pltpu.make_async_copy(piece, piece, gz_rs.at[b, h]).wait()
        if k >= 2:
            plane_drain(gsend, k - 2, Gx, g_ss, g_rs)
            plane_arrived(k - 2, Gx, g_rs, (0,))
        pack(gz, b, gsend, k)
        plane_send(gsend, k, Gx, g_ss, g_rs)

    steps = {
        "R": receive, "P": pack_tokens, "J": project, "B": give_back, "G": pack_grads,
        "S": lambda k: gz_copy(k, 0).start(), "s": lambda k: gz_copy(k, 1).start(),
    }

    def follow(plan):
        for name, k in plan:
            steps[name](k)

    ends, middle = plans(Z)
    if ends == middle:
        follow(ends)
    else:
        pl.when(~inner)(lambda: follow(ends))
        pl.when(inner)(lambda: follow(middle))

    for send, dst, ss, rs in ((psend, X, x_ss, x_rs), (gsend, Gx, g_ss, g_rs), (ysend, Yx, y_ss, y_rs)):
        for k in range(max(Z - 2, 0), Z):
            plane_drain(send, k, dst, ss, rs)
    for k in range(Z):
        plane_arrived(k, Gx, g_rs, range(0 if k >= Z - 2 else 1, E))
    gradient(X, Gx, 0, gw)

    for h in range(H):
        @pl.when(d > 0)
        def _():
            tok_copy(tokens, d, h, 0).wait_send()

        @pl.when(d < Z - 1)
        def _():
            tok_copy(tokens, d, h, 1).wait_send()

        for k in range(1, Z):
            b = block(k)

            @pl.when((b < d) & (d < Z - 1))
            def _():
                tok_copy(tok.at[b], b, h, 1).wait_send()

            @pl.when((b > d) & (d > 0))
            def _():
                tok_copy(tok.at[b], b, h, 0).wait_send()

    for k in range(1, Z):
        tgt_copy(k).wait_send()
        for h in range(2):
            gz_copy(k, h).wait_send()
    u_copy(0).wait()
    for k in range(1, Z):
        u_copy(k).wait_send()
        b = block(k)
        piece = out.at[:, pl.ds(pl.multiple_of(b * F, 128), F)]
        pltpu.make_async_copy(piece, piece, u_rs.at[b]).wait()


def place(n, rows_in, gw_in, X, Gx, rows_out, gw_out, rest, sems):
    head, F = gw_in.shape
    step = head // n
    copies = []
    for i in range(n):
        part = pl.ds(i * step, step)
        copies.append(pltpu.make_async_copy(gw_in.at[part], gw_out.at[part], sems.at[i]))
    copies.append(pltpu.make_async_copy(rows_in, rows_out, sems.at[n]))
    for copy in copies:
        copy.start()
    tm = 256
    tail = [
        pltpu.make_async_copy(rest.at[pl.ds(i * tm, tm)], gw_out.at[pl.ds(head + i * tm, tm)], sems.at[n + 1 + i])
        for i in range(rest.shape[0] // tm)
    ]
    for i, copy in enumerate(tail):
        gradient(X, Gx, head + i * tm, rest.at[pl.ds(i * tm, tm)])
        copy.start()
    for copy in copies + tail:
        copy.wait()


def local(Z, E, tokens, route, w_up, grad_up):
    R, D = tokens.shape
    w = w_up[0]
    F = w.shape[1]
    FF = grad_up.shape[1]
    C = -(-(9 * R // (8 * E)) // 8) * 8
    EC = E * C
    dma = pltpu.SemaphoreType.DMA
    any_spec = pl.BlockSpec(memory_space=pl.ANY)
    flops = 4 * Z * EC * D * F
    vmem = pl.BlockSpec(memory_space=pltpu.VMEM)
    late = LATE * 256
    out, gw, X, Gx = pl.pallas_call(
        functools.partial(kernel, Z, E, C),
        out_shape=(
            pltpu.VMEM((R, FF), BF16),
            pltpu.VMEM((D - late, F), BF16),
            pltpu.VMEM((Z * EC // 8, 8, D), BF16),
            pltpu.VMEM((Z * EC // 8, 8, F), BF16),
        ),
        in_specs=[any_spec] * 4,
        out_specs=(any_spec, vmem, vmem, vmem),
        scratch_shapes=[
            pltpu.VMEM((Z, R, D), BF16),
            pltpu.VMEM((Z, 8, R), F32),
            pltpu.VMEM((Z, R, F), BF16),
            pltpu.VMEM((D, F), BF16),
            pltpu.VMEM((Z * EC // 8, 8, F), BF16),
            pltpu.VMEM((2, E, C // 8, 8, D), BF16),
            pltpu.VMEM((2, E, C // 8, 8, F), BF16),
            pltpu.VMEM((2, E, C // 8, 8, F), BF16),
            pltpu.VMEM((Z, R, F), BF16),
            pltpu.VMEM((1, R), jnp.int32),
            dma((Z, H, 2)), dma((Z, H)), dma((Z,)), dma((Z,)), dma((Z, 2)), dma((Z, 2)),
            dma((2, E)), dma((Z, E)), dma((2, E)), dma((Z, E)), dma((2, E)), dma((Z, E)),
            dma((Z,)), dma((Z,)), dma((1,)), dma((4,)),
        ],
        compiler_params=pltpu.CompilerParams(
            collective_id=0, has_side_effects=True, vmem_limit_bytes=36 * 1024 * 1024
        ),
        cost_estimate=pl.CostEstimate(flops=flops, bytes_accessed=2 * D * F, transcendentals=0),
    )(*(pltpu.with_memory_space_constraint(a, pltpu.HBM) for a in (tokens, route.reshape(1, R), w, grad_up)))
    parts = 8
    rows, grad = pl.pallas_call(
        functools.partial(place, parts),
        out_shape=(jax.ShapeDtypeStruct((R, FF), BF16), jax.ShapeDtypeStruct((D, F), BF16)),
        in_specs=[any_spec, any_spec, vmem, vmem],
        out_specs=(any_spec, any_spec),
        scratch_shapes=[pltpu.VMEM((late, F), BF16), dma((parts + 1 + LATE,))],
        compiler_params=pltpu.CompilerParams(vmem_limit_bytes=16 * 1024 * 1024),
    )(*(pltpu.with_memory_space_constraint(a, pltpu.VMEM) for a in (out, gw, X, Gx)))
    return rows, grad[None]


def solution(mesh):
    rows = P(("groups", "dp", "expert"), None)
    return jax.shard_map(
        functools.partial(local, mesh.shape["dp"], mesh.shape["expert"]),
        mesh=mesh,
        in_specs=(rows, rows, P("expert", None, "dp"), rows),
        out_specs=(rows, P(("groups", "expert"), None, "dp")),
        check_vma=False,
    )
```

```python
import functools

import jax
import jax.numpy as jnp
from jax import lax
from jax.experimental import pallas as pl
from jax.experimental.pallas import tpu as pltpu
from jax.sharding import PartitionSpec as P

MESH = pl.DeviceIdType.MESH
BF16 = jnp.bfloat16
F32 = jnp.float32
H = 2
LATE = 5


def chunk_of(width):
    return 512 if width % 512 == 0 else width


def flat(ref, first, count, cols):
    return ref[pl.ds(first // 8, count // 8), :, cols].reshape(count, -1)


def gradient(X, Gx, first, gw, after=None):
    rows, F = gw.shape
    K = X.shape[0] * 8
    tm = 256 if rows % 256 == 0 else rows
    step = chunk_of(F)

    def body(i, _):
        at = pl.ds(pl.multiple_of(i * tm, tm), tm)
        xt = flat(X, 0, K, pl.ds(pl.multiple_of(first + i * tm, 128), tm)).T
        for n in range(F // step):
            cols = slice(n * step, (n + 1) * step)
            gw[at, cols] = jnp.dot(xt, flat(Gx, 0, K, cols), preferred_element_type=F32).astype(BF16)
        if after is not None:
            after(i)
        return 0

    lax.fori_loop(0, rows // tm, body, 0)


def plans(Z):
    if Z == 4:
        texts = (
            "R0G0P0R1J0P1B0S1s1J1R2P2S2s2B1G1J2S3s3G2B2R3P3J3G3B3",
            "R0P0J0S1s1G0R1P1S2R2s2B0P2S3s3R3J1J2B1P3B2G1G2J3B3G3",
        )
        return [[(text[i], int(text[i + 1])) for i in range(0, len(text), 2)] for text in texts]
    plan = [(name, 0) for name in "RPJGB"]
    for k in range(1, Z):
        plan += [(name, k) for name in "RSsPJB"]
    plan += [("G", k) for k in range(1, Z)]
    return [plan, plan]


def kernel(
    Z, E, C,
    tokens, route, w_hbm, grads,
    out, gw, X, Gx,
    tok, tgt, gz, w, Yx, psend, gsend, ysend, usend, rv,
    tok_ss, tok_rs, tgt_ss, tgt_rs, gz_ss, gz_rs,
    x_ss, x_rs, g_ss, g_rs, y_ss, y_rs, u_ss, u_rs, loc, wsem,
):
    R, D = tokens.shape
    F = w_hbm.shape[1]
    RH = R // H
    d = lax.axis_index("dp")
    me = lax.axis_index("expert")
    EC = E * C
    T = C // 8
    low = jnp.minimum(d, Z - 1 - d)
    inner = low > 0

    def block(k):
        if k == 0:
            return d
        near = d + (k + 1) // 2 if k % 2 else d - k // 2
        far = jnp.where(d <= Z - 1 - d, k, Z - 1 - k)
        return jnp.where(k <= 2 * low, near, far)

    barrier = pltpu.get_barrier_semaphore()
    for j in range(1, Z):
        pl.semaphore_signal(barrier, inc=1, device_id={"dp": lax.rem(d + j, Z)}, device_id_type=MESH)
    for j in range(1, E):
        pl.semaphore_signal(barrier, inc=1, device_id={"expert": lax.rem(me + j, E)}, device_id_type=MESH)
    rcopy = pltpu.make_async_copy(route, rv, wsem.at[1])
    rcopy.start()
    owntok = pltpu.make_async_copy(tokens, tok.at[d], wsem.at[2])
    owntok.start()
    pl.semaphore_wait(barrier, Z - 1 + E - 1)

    def half(h):
        return pl.ds(h * RH, RH)

    def tok_copy(src, b, h, side):
        return pltpu.make_async_remote_copy(
            src_ref=src.at[half(h)], dst_ref=tok.at[b, half(h)],
            send_sem=tok_ss.at[b, h, side], recv_sem=tok_rs.at[b, h],
            device_id={"dp": d - 1 if side == 0 else d + 1}, device_id_type=MESH)

    for h in range(H):
        @pl.when(d > 0)
        def _():
            tok_copy(tokens, d, h, 0).start()

        @pl.when(d < Z - 1)
        def _():
            tok_copy(tokens, d, h, 1).start()

    wcopy = pltpu.make_async_copy(w_hbm, w, wsem.at[0])
    wcopy.start()
    owngrad = pltpu.make_async_copy(grads.at[:, pl.ds(pl.multiple_of(d * F, 128), F)], gz.at[d], wsem.at[3])
    owngrad.start()

    rcopy.wait()
    row = jnp.broadcast_to(rv[...], (R, R))
    ri = lax.broadcasted_iota(jnp.int32, (R, R), 0)
    ci = lax.broadcasted_iota(jnp.int32, (R, R), 1)
    col = jnp.sum(jnp.where(ri == ci, row, 0), axis=1, keepdims=True)
    rank = jnp.sum(jnp.where((col == row) & (ri < ci), 1, 0), axis=0, keepdims=True)
    slot = (rv[...] * C + rank).astype(F32)
    tgt[d] = jnp.broadcast_to(slot, (8, R))

    def tgt_copy(j):
        return pltpu.make_async_remote_copy(
            src_ref=tgt.at[d], dst_ref=tgt.at[d], send_sem=tgt_ss.at[j], recv_sem=tgt_rs.at[d],
            device_id={"dp": lax.rem(d + j, Z)}, device_id_type=MESH)

    for j in range(1, Z):
        tgt_copy(j).start()

    def one_hot(b):
        t = tgt[b][0:1].astype(jnp.int32)
        s = lax.broadcasted_iota(jnp.int32, (EC, R), 0)
        return jnp.where(s == t, 1.0, 0.0).astype(BF16)

    def receive(k):
        if k == 0:
            owntok.wait()
            return
        b = block(k)
        for h in range(H):
            piece = tok.at[b, half(h)]
            pltpu.make_async_copy(piece, piece, tok_rs.at[b, h]).wait()

            @pl.when((b < d) & (d < Z - 1))
            def _():
                tok_copy(tok.at[b], b, h, 1).start()

            @pl.when((b > d) & (d > 0))
            def _():
                tok_copy(tok.at[b], b, h, 0).start()
        pltpu.make_async_copy(tgt.at[b], tgt.at[b], tgt_rs.at[b]).wait()

    def gz_copy(k, h):
        to = block(k)
        rows = pl.ds(h * (R // 2), R // 2)
        return pltpu.make_async_remote_copy(
            src_ref=grads.at[rows, pl.ds(pl.multiple_of(to * F, 128), F)], dst_ref=gz.at[d, rows],
            send_sem=gz_ss.at[k, h], recv_sem=gz_rs.at[d, h], device_id={"dp": to}, device_id_type=MESH)

    def rows_at(b, e):
        return pl.ds((b * E + e) * T, T)

    def plane_copy(send, k, j, dst, b, ss, rs):
        to = lax.rem(me + j, E)
        if j == 0:
            return pltpu.make_async_copy(send.at[k % 2, to], dst.at[rows_at(b, me)], rs.at[b, 0])
        return pltpu.make_async_remote_copy(
            src_ref=send.at[k % 2, to], dst_ref=dst.at[rows_at(b, me)],
            send_sem=ss.at[k % 2, j], recv_sem=rs.at[b, j], device_id={"expert": to}, device_id_type=MESH)

    def plane_send(send, k, dst, ss, rs):
        for j in list(range(1, E)) + [0]:
            plane_copy(send, k, j, dst, block(k), ss, rs).start()

    def plane_drain(send, k, dst, ss, rs):
        for j in range(1, E):
            plane_copy(send, k, j, dst, block(k), ss, rs).wait_send()

    def plane_arrived(k, dst, rs, offsets=None):
        b = block(k)
        for j in offsets or range(E):
            piece = dst.at[rows_at(b, 0)]
            pltpu.make_async_copy(piece, piece, rs.at[b, j]).wait()

    def pack(src, b, send, k):
        oh = one_hot(b)
        width = src.shape[-1]
        step = chunk_of(width)

        def body(i, _):
            cols = pl.ds(pl.multiple_of(i * step, step), step)
            r = jnp.dot(oh, src[b, :, cols], preferred_element_type=F32)
            for e in range(E):
                send[k % 2, e, :, :, cols] = r[e * C:(e + 1) * C].astype(BF16).reshape(T, 8, -1)
            return 0

        lax.fori_loop(0, width // step, body, 0)

    def pack_tokens(k):
        if k >= 2:
            plane_drain(psend, k - 2, X, x_ss, x_rs)
        pack(tok, block(k), psend, k)
        plane_send(psend, k, X, x_ss, x_rs)

    def project(k):
        b = block(k)
        plane_arrived(k, X, x_rs)
        if k >= 2:
            plane_drain(ysend, k - 2, Yx, y_ss, y_rs)
        if k == 0:
            wcopy.wait()
        step = chunk_of(F)

        def body(i, _):
            cols = pl.ds(pl.multiple_of(i * step, step), step)
            r = jnp.dot(flat(X, b * EC, EC, slice(None)), w[:, cols], preferred_element_type=F32)
            for e in range(E):
                ysend[k % 2, e, :, :, cols] = r[e * C:(e + 1) * C].astype(BF16).reshape(T, 8, -1)
            return 0

        lax.fori_loop(0, F // step, body, 0)
        plane_send(ysend, k, Yx, y_ss, y_rs)

    def u_copy(k):
        b = block(k)
        cols = pl.ds(pl.multiple_of(d * F, 128), F)
        if k == 0:
            return pltpu.make_async_copy(usend.at[0], out.at[:, cols], loc.at[0])
        return pltpu.make_async_remote_copy(
            src_ref=usend.at[k], dst_ref=out.at[:, cols], send_sem=u_ss.at[k], recv_sem=u_rs.at[d],
            device_id={"dp": b}, device_id_type=MESH)

    def give_back(k):
        b = block(k)
        plane_arrived(k, Yx, y_rs)
        oh = one_hot(b)
        step = chunk_of(F)

        def body(i, _):
            cols = pl.ds(pl.multiple_of(i * step, step), step)
            r = lax.dot_general(oh, flat(Yx, b * EC, EC, cols), (((0,), (0,)), ((), ())), preferred_element_type=F32)
            usend[k, :, cols] = r.astype(BF16)
            return 0

        lax.fori_loop(0, F // step, body, 0)
        u_copy(k).start()

    def pack_grads(k):
        b = block(k)
        if k == 0:
            owngrad.wait()
        else:
            for h in range(2):
                piece = gz.at[b, pl.ds(h * (R // 2), R // 2)]
                pltpu.make_async_copy(piece, piece, gz_rs.at[b, h]).wait()
        if k >= 2:
            plane_drain(gsend, k - 2, Gx, g_ss, g_rs)
            plane_arrived(k - 2, Gx, g_rs, (0,))
        pack(gz, b, gsend, k)
        plane_send(gsend, k, Gx, g_ss, g_rs)

    steps = {
        "R": receive, "P": pack_tokens, "J": project, "B": give_back, "G": pack_grads,
        "S": lambda k: gz_copy(k, 0).start(), "s": lambda k: gz_copy(k, 1).start(),
    }

    def follow(plan):
        for name, k in plan:
            steps[name](k)

    ends, middle = plans(Z)
    if ends == middle:
        follow(ends)
    else:
        pl.when(~inner)(lambda: follow(ends))
        pl.when(inner)(lambda: follow(middle))

    for send, dst, ss, rs in ((psend, X, x_ss, x_rs), (gsend, Gx, g_ss, g_rs), (ysend, Yx, y_ss, y_rs)):
        for k in range(max(Z - 2, 0), Z):
            plane_drain(send, k, dst, ss, rs)
    for k in range(Z):
        plane_arrived(k, Gx, g_rs, range(0 if k >= Z - 2 else 1, E))
    gradient(X, Gx, 0, gw)

    for h in range(H):
        @pl.when(d > 0)
        def _():
            tok_copy(tokens, d, h, 0).wait_send()

        @pl.when(d < Z - 1)
        def _():
            tok_copy(tokens, d, h, 1).wait_send()

        for k in range(1, Z):
            b = block(k)

            @pl.when((b < d) & (d < Z - 1))
            def _():
                tok_copy(tok.at[b], b, h, 1).wait_send()

            @pl.when((b > d) & (d > 0))
            def _():
                tok_copy(tok.at[b], b, h, 0).wait_send()

    for k in range(1, Z):
        tgt_copy(k).wait_send()
        for h in range(2):
            gz_copy(k, h).wait_send()
    u_copy(0).wait()
    for k in range(1, Z):
        u_copy(k).wait_send()
        b = block(k)
        piece = out.at[:, pl.ds(pl.multiple_of(b * F, 128), F)]
        pltpu.make_async_copy(piece, piece, u_rs.at[b]).wait()


def place(n, rows_in, gw_in, X, Gx, rows_out, gw_out, rest, sems):
    head, F = gw_in.shape
    step = head // n
    copies = []
    for i in range(n):
        part = pl.ds(i * step, step)
        copies.append(pltpu.make_async_copy(gw_in.at[part], gw_out.at[part], sems.at[i]))
    copies.append(pltpu.make_async_copy(rows_in, rows_out, sems.at[n]))
    for copy in copies:
        copy.start()
    tm = 256
    tail = [
        pltpu.make_async_copy(rest.at[pl.ds(i * tm, tm)], gw_out.at[pl.ds(head + i * tm, tm)], sems.at[n + 1 + i])
        for i in range(rest.shape[0] // tm)
    ]
    for i, copy in enumerate(tail):
        gradient(X, Gx, head + i * tm, rest.at[pl.ds(i * tm, tm)])
        copy.start()
    for copy in copies + tail:
        copy.wait()


def local(Z, E, tokens, route, w_up, grad_up):
    R, D = tokens.shape
    w = w_up[0]
    F = w.shape[1]
    FF = grad_up.shape[1]
    C = -(-(9 * R // (8 * E)) // 8) * 8
    EC = E * C
    dma = pltpu.SemaphoreType.DMA
    any_spec = pl.BlockSpec(memory_space=pl.ANY)
    flops = 4 * Z * EC * D * F
    vmem = pl.BlockSpec(memory_space=pltpu.VMEM)
    late = LATE * 256
    out, gw, X, Gx = pl.pallas_call(
        functools.partial(kernel, Z, E, C),
        out_shape=(
            pltpu.VMEM((R, FF), BF16),
            pltpu.VMEM((D - late, F), BF16),
            pltpu.VMEM((Z * EC // 8, 8, D), BF16),
            pltpu.VMEM((Z * EC // 8, 8, F), BF16),
        ),
        in_specs=[any_spec] * 4,
        out_specs=(any_spec, vmem, vmem, vmem),
        scratch_shapes=[
            pltpu.VMEM((Z, R, D), BF16),
            pltpu.VMEM((Z, 8, R), F32),
            pltpu.VMEM((Z, R, F), BF16),
            pltpu.VMEM((D, F), BF16),
            pltpu.VMEM((Z * EC // 8, 8, F), BF16),
            pltpu.VMEM((2, E, C // 8, 8, D), BF16),
            pltpu.VMEM((2, E, C // 8, 8, F), BF16),
            pltpu.VMEM((2, E, C // 8, 8, F), BF16),
            pltpu.VMEM((Z, R, F), BF16),
            pltpu.VMEM((1, R), jnp.int32),
            dma((Z, H, 2)), dma((Z, H)), dma((Z,)), dma((Z,)), dma((Z, 2)), dma((Z, 2)),
            dma((2, E)), dma((Z, E)), dma((2, E)), dma((Z, E)), dma((2, E)), dma((Z, E)),
            dma((Z,)), dma((Z,)), dma((1,)), dma((4,)),
        ],
        compiler_params=pltpu.CompilerParams(
            collective_id=0, has_side_effects=True, vmem_limit_bytes=36 * 1024 * 1024
        ),
        cost_estimate=pl.CostEstimate(flops=flops, bytes_accessed=2 * D * F, transcendentals=0),
    )(*(pltpu.with_memory_space_constraint(a, pltpu.HBM) for a in (tokens, route.reshape(1, R), w, grad_up)))
    parts = 8
    rows, grad = pl.pallas_call(
        functools.partial(place, parts),
        out_shape=(jax.ShapeDtypeStruct((R, FF), BF16), jax.ShapeDtypeStruct((D, F), BF16)),
        in_specs=[any_spec, any_spec, vmem, vmem],
        out_specs=(any_spec, any_spec),
        scratch_shapes=[pltpu.VMEM((late, F), BF16), dma((parts + 1 + LATE,))],
        compiler_params=pltpu.CompilerParams(vmem_limit_bytes=16 * 1024 * 1024),
    )(*(pltpu.with_memory_space_constraint(a, pltpu.VMEM) for a in (out, gw, X, Gx)))
    return rows, grad[None]


def solution(mesh):
    rows = P(("groups", "dp", "expert"), None)
    return jax.shard_map(
        functools.partial(local, mesh.shape["dp"], mesh.shape["expert"]),
        mesh=mesh,
        in_specs=(rows, rows, P("expert", None, "dp"), rows),
        out_specs=(rows, P(("groups", "expert"), None, "dp")),
        check_vma=False,
    )
```
